32 devices in a mesh: dp: 4 (over y, core), tensor: 8 (over z, x).
Axes of the slice: x: 2, y: 2, z: 4, core: 2. Of those that a mesh axis runs over, the one named last changes fastest.
Arguments:
- tokens: bfloat16 [3072, 8192], P('dp', 'tensor'), may hold values from -6 to 6
- cotangent: bfloat16 [3072, 512], P('dp', 'tensor'), may hold values from -0.0625 to 0.0625
- frozen_value_weight: bfloat16 [8192, 512], P('tensor'), may hold values from -0.0625 to 0.0625
- adapter_down_weight: bfloat16 [8, 32, 8192], P('tensor'), may hold values from -0.0625 to 0.0625
- adapter_up_weight: bfloat16 [8, 32, 512], P('tensor'), may hold values from -1 to 1
- member: int32 [24, 1], P('dp'), may hold values from 0 to 7; in each aligned block of 6 rows (0 to 5, 6 to 11, ...) at most 2 rows name the same one
Outputs:
- output: bfloat16 [3072, 512], P(('dp', 'tensor'))
- grad_down: float32 [8, 32, 8192], P('tensor', None, 'dp')
- grad_up: float32 [8, 32, 512], P('tensor', 'dp')
The draws below stay inside these ranges and needn't reach their ends.
Inputs may be any that keep to these rules, and one draw needn't show every extreme that they name: Within the 6 blocks of one data index no member appears more than 2 times, and some member appears exactly 2 times there.
All inputs are finite; a program needn't handle non-finite values.
Results may differ from the reference program's by a relative error of at most 0.015.
Values may be sent and summed in bfloat16 or wider, within the bound.
A program may use at most 64 MiB of HBM per device.

```python
import math
import jax
import jax.numpy as jnp
import numpy as np
from jax import lax

MODEL_WIDTH = 8192
VALUE_FEATURES = 512
ADAPTER_RANK = 32
BLK = 128
CAP = 2
MEMBER_COUNT = 8
NB = 6
ROWS = 768
TOKENS = 3072
N_DP = 4
N_TENSOR = 8


def raised(array, key, source, target, blocks, factor):
    def block_of(dim):
        return (jnp.arange(array.shape[dim]) // (array.shape[dim] // blocks)).reshape((-1,) + (1,) * (array.ndim - 1 - dim))

    near = jax.random.permutation(key, blocks)[block_of(target)]
    far = (block_of(target) + blocks // 2) % blocks
    return jnp.where((block_of(source) == near) | (block_of(source) == far), factor * array, array)


def shard_levels(stream_key, dims, pieces, least, high):
    level, own = 1.0, jax.random.fold_in(stream_key, 6)
    for position, blocks in pieces:
        draws = jnp.exp(jax.random.uniform(jax.random.fold_in(own, position), (blocks,), jnp.float32, least / len(pieces), high / len(pieces)))
        level = level * jnp.repeat(draws, dims[position] // blocks).reshape([-1 if axis == position else 1 for axis in range(len(dims))])
    return level


def deal_out(key, own, number, rows, amount, top, most, slope):
    ranking = jax.random.permutation(key, amount)
    packed, usual = load_shares(amount, rows * top, most, slope, True), load_shares(amount, rows * top, most, slope, False)
    places = jnp.arange(amount)

    def named(sizes, rotation):
        used = int((sizes > 0).sum())
        fixed = max(1, used // 4)
        passed = fixed + (places - fixed + rotation * (used - fixed)) % max(1, amount - fixed)
        return jnp.zeros((amount,), jnp.int32).at[ranking[jnp.where(places < fixed, places, passed)]].set(jnp.asarray(sizes, jnp.int32))

    sizes = jnp.where(number % 4 == 0, named(packed, number // 4), named(usual, number - number // 4 - 1))
    mixed = jax.random.permutation(jax.random.fold_in(own, 3), amount)
    source_of, taker = mixed[0:amount // 2 * 2:2], mixed[1:amount // 2 * 2:2]
    room = jnp.minimum(sizes[source_of] - 1, most - sizes[taker]) // 2
    room = jnp.where((source_of == ranking[0]) | (taker == ranking[0]) | (sizes[taker] == 0), 0, jnp.maximum(room, 0))
    passed = jax.random.randint(jax.random.fold_in(own, 4), (amount // 2,), 0, 1 << 20) % (room + 1)
    sizes = sizes.at[source_of].add(-passed).at[taker].add(passed)
    items = jnp.searchsorted(jnp.cumsum(sizes), jnp.arange(rows * top), side="right").astype(jnp.int32)
    grid = items.reshape(top, rows).T
    grid = grid[jax.random.permutation(jax.random.fold_in(own, 1), rows)]
    rotation = jax.random.randint(jax.random.fold_in(own, 2), (rows, 1), 0, top)
    return jnp.take_along_axis(grid, (jnp.arange(top)[None, :] + rotation) % top, axis=1)


def load_shares(count, total, limit, lean, full):
    weights = [(1 << 20) // math.isqrt(rank ** lean) + 1 for rank in range(1, count + 1)]
    largest = limit if full else min(limit, max(-(-total // count), total * weights[0] // sum(weights)))
    least = 1 if total - largest >= count - 1 else 0
    holding, rest = [largest] + [least] * (count - 1), total - largest - least * (count - 1)
    while rest > 0:
        free = [i for i in range(1, count) if holding[i] < largest] or [i for i in range(1, count) if holding[i] < limit]
        whole, budget = sum([weights[i] for i in free]), rest
        for i in free:
            more = min(limit - holding[i], max(1, budget * weights[i] // whole), rest)
            holding[i] = holding[i] + more
            rest = rest - more
    return np.array(holding)


def gaussian(key, extent, spread, most, shards=(), held_as=jnp.bfloat16):
    level = shard_levels(key, extent, shards, -0.22, 0.18) if shards else 1.0
    values = jax.random.normal(key, extent, jnp.float32) * spread * level
    return jnp.minimum(jnp.maximum(values, -most), most).astype(held_as)


def noise_with(key, extent, scale, limit, pieces, heavy, dtype=jnp.bfloat16):
    values = scale * jax.random.normal(key, extent, jnp.float32)
    if pieces:
        values = values * shard_levels(key, extent, pieces, -0.22, 0.18)
    return jnp.clip(raised(values, jax.random.fold_in(key, 3), *heavy), -limit, limit).astype(dtype)


def setup_inputs(seed: int = 0) -> dict:
    keys = jax.random.split(jax.random.key(seed), 7)
    tokens = noise_with(keys[0], (TOKENS, MODEL_WIDTH), 1.0, 6.0, ((0, 4), (1, 8)), (1, 0, 8, 2.0))
    cotangent = gaussian(keys[1], (TOKENS, VALUE_FEATURES), (0.25 / (BLK * N_DP) ** 0.5), 0.0625, ((0, 4), (1, 8)))
    frozen_value_weight = gaussian(keys[2], (MODEL_WIDTH, VALUE_FEATURES), MODEL_WIDTH ** -0.5, 0.0625, ((0, 8),))
    adapter_down_weight = gaussian(keys[3], (MEMBER_COUNT, ADAPTER_RANK, MODEL_WIDTH), MODEL_WIDTH ** -0.5, 0.0625, ((0, 8),))
    adapter_up_weight = gaussian(keys[4], (MEMBER_COUNT, ADAPTER_RANK, VALUE_FEATURES), ADAPTER_RANK ** -0.5, 1.0, ((0, 8),))
    member_keys = jax.random.split(jax.random.fold_in(keys[5], 1), (NB * N_DP) // NB)
    member_turns = jax.random.permutation(jax.random.fold_in(keys[5], 3), (NB * N_DP) // NB)
    member = jax.vmap(lambda own, number: deal_out(jax.random.fold_in(keys[5], 2), own, number, NB, MEMBER_COUNT, 1, CAP, 2))(member_keys, member_turns).reshape((NB * N_DP, 1))
    return dict(tokens=tokens, cotangent=cotangent, frozen_value_weight=frozen_value_weight, adapter_down_weight=adapter_down_weight, adapter_up_weight=adapter_up_weight, member=member)


adapter_scale = 2.0
contract_trailing = (((1,), (1,)), ((), ()))
contract_leading = (((0,), (0,)), ((), ()))


def reference(tokens, cotangent, frozen_value_weight, adapter_down_weight, adapter_up_weight, member):
    feature_width = MODEL_WIDTH // N_TENSOR
    slice_weights = frozen_value_weight.reshape(N_TENSOR, feature_width, VALUE_FEATURES)
    group_tokens = tokens.reshape(N_DP, ROWS, MODEL_WIDTH)
    group_cot = cotangent.reshape(N_DP, ROWS, VALUE_FEATURES)
    group_ids = member.reshape(N_DP, NB).astype(jnp.int32)

    def group_step(totals, group_item):
        these_tokens, these_cot, these_ids = group_item
        sliced = these_tokens.reshape(ROWS, N_TENSOR, feature_width).transpose(1, 0, 2)

        def add_slice(running, paired):
            feature_piece, weight_piece = paired
            partial_sum = jnp.dot(feature_piece, weight_piece, preferred_element_type=jnp.float32).astype(jnp.bfloat16)
            partial_sum = lax.optimization_barrier(partial_sum)
            return running + partial_sum.astype(jnp.float32), None

        base_total, _ = lax.scan(add_slice, jnp.zeros((ROWS, VALUE_FEATURES), jnp.float32), (sliced, slice_weights))
        block_tokens = these_tokens.reshape(NB, BLK, MODEL_WIDTH)
        block_cots = these_cot.reshape(NB, BLK, VALUE_FEATURES)

        def block_step(grads, block_item):
            grad_a, grad_b = grads
            block_rows, block_cotangent, current_member = block_item
            down_projection = adapter_down_weight[current_member]
            up_projection = adapter_up_weight[current_member]
            hidden_state = lax.dot_general(block_rows, down_projection, contract_trailing, preferred_element_type=jnp.float32).astype(jnp.bfloat16)
            adapter_result = (adapter_scale * jnp.dot(hidden_state, up_projection, preferred_element_type=jnp.float32)).astype(jnp.bfloat16)
            backward_projection = (adapter_scale * lax.dot_general(block_cotangent, up_projection, contract_trailing, preferred_element_type=jnp.float32)).astype(jnp.bfloat16)
            term_down = lax.dot_general(backward_projection, block_rows, contract_leading, preferred_element_type=jnp.float32)
            up_term_value = adapter_scale * lax.dot_general(hidden_state, block_cotangent, contract_leading, preferred_element_type=jnp.float32)
            grad_a = grad_a.at[current_member].add(term_down)
            grad_b = grad_b.at[current_member].add(up_term_value)
            return (grad_a, grad_b), adapter_result

        start_grads = (jnp.zeros((MEMBER_COUNT, ADAPTER_RANK, MODEL_WIDTH), jnp.float32), jnp.zeros((MEMBER_COUNT, ADAPTER_RANK, VALUE_FEATURES), jnp.float32))
        (group_down, group_up), outs = lax.scan(block_step, start_grads, (block_tokens, block_cots, these_ids))
        output_rows = (base_total + outs.reshape(ROWS, VALUE_FEATURES).astype(jnp.float32)).astype(jnp.bfloat16)
        round_down = lax.optimization_barrier(group_down.astype(jnp.bfloat16))
        round_up = lax.optimization_barrier(group_up.astype(jnp.bfloat16))
        totals = (totals[0] + round_down.astype(jnp.float32), totals[1] + round_up.astype(jnp.float32))
        return totals, output_rows

    start_totals = (jnp.zeros((MEMBER_COUNT, ADAPTER_RANK, MODEL_WIDTH), jnp.float32), jnp.zeros((MEMBER_COUNT, ADAPTER_RANK, VALUE_FEATURES), jnp.float32))
    (grad_down, grad_up), outputs = lax.scan(group_step, start_totals, (group_tokens, group_cot, group_ids))
    return outputs.reshape(TOKENS, VALUE_FEATURES), grad_down, grad_up
```

```python
import functools

import jax
import jax.numpy as jnp
from jax import lax
from jax.experimental import pallas as pl
from jax.experimental.pallas import tpu as pltpu
from jax.sharding import PartitionSpec as P

BLK = 128
SCALE = 2.0
TRAIL = (((1,), (1,)), ((), ()))
LEAD = (((0,), (0,)), ((), ()))
F32 = jnp.float32
BF16 = jnp.bfloat16


def kernel(n, dp, member, tok, cot, w, down, up, out, gdown, gup, dw, uw, ms, mr, hb, gs, gr, us, ur,
           wd_s, wd_r, wu_s, wu_r, fd_s, fd_r, fu_s, fu_r, m_s, m_r, h_s, h_r, g_s, g_r, u_s, u_r):
    d = lax.axis_index("dp")
    j = lax.axis_index("tensor")
    total = dp * n
    lin = d * n + j
    _, rows, feat = tok.shape
    cw = cot.shape[2]
    rank, width = up.shape
    half = rank // 2
    per = n // dp
    core = d % 2
    mate = d + 1 - 2 * core
    blocks = member.shape[0]
    mine = pl.ds(pl.multiple_of(core * half, half), half)
    other = pl.ds(pl.multiple_of((1 - core) * half, half), half)

    def rcopy(src, dst, s, r, dd, tt):
        return pltpu.make_async_remote_copy(
            src_ref=src, dst_ref=dst, send_sem=s, recv_sem=r,
            device_id={"dp": dd, "tensor": tt}, device_id_type=pl.DeviceIdType.MESH)

    def loop(lo, hi, fn):
        def step(k, c):
            fn(k)
            return c
        lax.fori_loop(lo, hi, step, 0)

    barrier = pltpu.get_barrier_semaphore()

    def greet(o):
        t = (lin + o) % total
        pl.semaphore_signal(barrier, inc=1, device_id={"dp": t // n, "tensor": t % n},
                            device_id_type=pl.DeviceIdType.MESH)

    loop(1, total, greet)
    dw[j] = down[:, pl.ds(pl.multiple_of(j * feat, feat), feat)]
    uw[j] = up[...]
    pl.semaphore_wait(barrier, total - 1)

    def down_copy(o):
        t = (j + o) % n
        return rcopy(down.at[mine, pl.ds(pl.multiple_of(t * feat, feat), feat)], dw.at[j, mine],
                     wd_s.at[o], wd_r.at[o], d, t)

    def up_copy(o):
        t = (j + o) % n
        return rcopy(up.at[mine], uw.at[j, mine], wu_s.at[o], wu_r.at[o], d, t)

    loop(1, n, lambda o: down_copy(o).start())
    loop(1, n, lambda o: up_copy(o).start())

    def base(i):
        ms[i, :, 0:width] = jnp.dot(tok[i], w[...], preferred_element_type=F32).astype(BF16)

    loop(0, n, base)

    def fdown(o, part):
        s = (j + n - o) % n
        return rcopy(dw.at[s, part], dw.at[s, part], fd_s.at[o], fd_r.at[o], mate, j)

    def fup(o, part):
        s = (j + n - o) % n
        return rcopy(uw.at[s, part], uw.at[s, part], fu_s.at[o], fu_r.at[o], mate, j)

    def got_down(o):
        s = (j + n - o) % n
        rcopy(dw.at[s, mine], dw.at[s, mine], wd_s.at[o], wd_r.at[o], d, s).wait_recv()
        fdown(o, mine).start()

    def got_up(o):
        s = (j + n - o) % n
        rcopy(uw.at[s, mine], uw.at[s, mine], wu_s.at[o], wu_r.at[o], d, s).wait_recv()
        fup(o, mine).start()

    loop(1, n, got_down)
    loop(1, n, got_up)
    loop(1, n, lambda o: fdown(o, other).wait_recv())
    loop(1, n, lambda o: fup(o, other).wait_recv())

    pick = (lax.broadcasted_iota(jnp.int32, (width, cw), 0)
            == lax.broadcasted_iota(jnp.int32, (width, cw), 1) + j * cw).astype(BF16)

    def owners(i):
        k0 = (i * rows) // BLK
        k1 = (i * rows + rows - 1) // BLK
        return member[k0], member[k1], (k0 + 1) * BLK - i * rows

    def msg(i, o):
        return rcopy(ms.at[i], mr.at[j], m_s.at[o], m_r.at[o], d, i)

    def split(x):
        hi = x.astype(BF16)
        return hi, (x - hi.astype(F32)).astype(BF16)

    def partial(o):
        i = (j + o) % n
        m0, m1, edge = owners(i)
        first = lax.broadcasted_iota(jnp.int32, (rows, rank), 0) < edge
        pair = jnp.concatenate([dw[m0], dw[m1]], axis=0)
        hs = lax.dot_general(tok[i], pair, TRAIL, preferred_element_type=F32)
        upair = jnp.concatenate([uw[m0], uw[m1]], axis=0)
        uj = jnp.dot(upair, pick, preferred_element_type=F32).astype(BF16)
        bs = SCALE * lax.dot_general(cot[i], uj, TRAIL, preferred_element_type=F32)
        h = jnp.where(first, hs[:, :rank], hs[:, rank:])
        b = jnp.where(first, bs[:, :rank], bs[:, rank:])
        ms[i, :, width:] = jnp.concatenate([*split(h), *split(b)], axis=1)

    def partial_send(o):
        partial(o)
        msg((j + o) % n, o).start()

    loop(1, n, partial_send)
    partial(0)

    def msg_recv(o):
        s = (j + n - o) % n
        rcopy(mr.at[s], mr.at[s], m_s.at[o], m_r.at[o], d, s).wait_recv()

    loop(1, n, msg_recv)
    mr[j] = ms[j]
    side = sum(mr[s, :, width:].astype(F32) for s in range(n))
    hidden = (side[:, :rank] + side[:, rank:2 * rank]).astype(BF16)
    back = (side[:, 2 * rank:3 * rank] + side[:, 3 * rank:]).astype(BF16)
    hb[j] = jnp.concatenate([hidden, back], axis=1)

    def hb_copy(o):
        return rcopy(hb.at[j], hb.at[j], h_s.at[o], h_r.at[o], d, (j + o) % n)

    loop(1, n, lambda o: hb_copy(o).start())

    m0, m1, edge = owners(j)
    a0 = SCALE * jnp.dot(hidden, uw[m0], preferred_element_type=F32)
    a1 = SCALE * jnp.dot(hidden, uw[m1], preferred_element_type=F32)
    first = lax.broadcasted_iota(jnp.int32, (rows, width), 0) < edge
    adapter = jnp.where(first, a0, a1).astype(BF16).astype(F32)
    base_total = sum(mr[s, :, :width].astype(F32) for s in range(n))
    out[...] = (base_total + adapter).astype(BF16)

    def hb_recv(o):
        s = (j + n - o) % n
        rcopy(hb.at[s], hb.at[s], h_s.at[o], h_r.at[o], d, s).wait_recv()

    loop(1, n, hb_recv)

    def flat(x):
        if rows % 16 == 0:
            return x.reshape(n * rows, x.shape[2])
        return x.astype(F32).reshape(n * rows, x.shape[2]).astype(BF16)

    both = flat(hb[...])
    span = n * rank
    row_block = lax.broadcasted_iota(jnp.int32, (n * rows, 1), 0) // BLK
    row_member = jnp.zeros((n * rows, 1), jnp.int32)
    for k in range(blocks):
        row_member = jnp.where(row_block == k, member[k], row_member)
    keep = lax.broadcasted_iota(jnp.int32, (n * rows, span), 1) // rank == row_member
    ra = lax.broadcasted_iota(jnp.int32, (2 * rank, span), 0)
    rb = lax.broadcasted_iota(jnp.int32, (2 * rank, span), 1) % rank

    def spread(offset):
        tiled = jnp.dot(both, (ra == rb + offset).astype(BF16), preferred_element_type=F32)
        return jnp.where(keep, tiled, 0.0).astype(BF16)

    gd = lax.dot_general(spread(rank), flat(tok[...]), LEAD, preferred_element_type=F32)
    gs[...] = gd.astype(BF16).reshape(n, rank, feat)

    dd, slot = j // per, d * per + j % per

    def gd_copy(m):
        return rcopy(gs.at[m], gr.at[slot], g_s.at[m], g_r.at[slot], dd, m)

    def not_me(m):
        return jnp.logical_or(dd != d, m != j)

    def gd_start(m):
        @pl.when(not_me(m))
        def _():
            gd_copy(m).start()

    loop(0, n, gd_start)

    @pl.when(dd == d)
    def _():
        gr[slot] = gs[j]

    gu = (SCALE * lax.dot_general(spread(0), flat(cot[...]), LEAD, preferred_element_type=F32))
    gu = gu.reshape(n, rank, cw)
    part = rank // dp
    for k in range(dp):
        us[:, k] = gu[:, k * part:(k + 1) * part, :]

    def gu_copy(o):
        t = (lin + o) % total
        return rcopy(us.at[t % n, t // n], ur.at[d, j], u_s.at[o], u_r.at[o], t // n, t % n)

    loop(1, total, lambda o: gu_copy(o).start())
    ur[d, j] = us[j, d]

    def gd_recv(k):
        sd, sj = k // per, d * per + k % per

        @pl.when(jnp.logical_or(sd != d, sj != j))
        def _():
            rcopy(gr.at[k], gr.at[k], g_s.at[0], g_r.at[k], sd, sj).wait_recv()

    loop(0, dp * per, gd_recv)
    for q in range(per):
        gdown[:, q * feat:(q + 1) * feat] = sum(gr[k * per + q].astype(F32) for k in range(dp))

    def gu_recv(o):
        s = (lin + total - o) % total
        rcopy(ur.at[s // n, s % n], ur.at[s // n, s % n], u_s.at[o], u_r.at[o], s // n, s % n).wait_recv()

    loop(1, total, gu_recv)
    gup[...] = jnp.concatenate([sum(ur[k, t] for k in range(dp)) for t in range(n)], axis=1)

    def drain(o):
        down_copy(o).wait_send()
        up_copy(o).wait_send()
        fdown(o, mine).wait_send()
        fup(o, mine).wait_send()
        msg((j + o) % n, o).wait_send()
        hb_copy(o).wait_send()

    loop(1, n, drain)

    def gd_drain(m):
        @pl.when(not_me(m))
        def _():
            gd_copy(m).wait_send()

    loop(0, n, gd_drain)
    loop(1, total, lambda o: gu_copy(o).wait_send())


def solution(mesh):
    dp, n = mesh.shape["dp"], mesh.shape["tensor"]

    def shards(tokens, cotangent, w, down, up, member):
        rows, feat = tokens.shape[0] // n, tokens.shape[1]
        cw, width, rank = cotangent.shape[1], w.shape[1], up.shape[1]
        per = n // dp
        vmem = pl.BlockSpec(memory_space=pltpu.VMEM)
        dma = lambda k: pltpu.SemaphoreType.DMA((k,))
        out, gdown, gup = pl.pallas_call(
            functools.partial(kernel, n, dp),
            out_shape=(
                jax.ShapeDtypeStruct((rows, width), BF16),
                jax.ShapeDtypeStruct((rank, per * feat), F32),
                jax.ShapeDtypeStruct((rank // dp, width), F32),
            ),
            in_specs=[pl.BlockSpec(memory_space=pltpu.SMEM)] + [vmem] * 5,
            out_specs=(vmem,) * 3,
            scratch_shapes=[
                pltpu.VMEM((n, rank, feat), BF16),
                pltpu.VMEM((n, rank, width), BF16),
                pltpu.VMEM((n, rows, width + 4 * rank), BF16),
                pltpu.VMEM((n, rows, width + 4 * rank), BF16),
                pltpu.VMEM((n, rows, 2 * rank), BF16),
                pltpu.VMEM((n, rank, feat), BF16),
                pltpu.VMEM((dp * per, rank, feat), BF16),
                pltpu.VMEM((n, dp, rank // dp, cw), F32),
                pltpu.VMEM((dp, n, rank // dp, cw), F32),
                *[dma(n) for _ in range(12)],
                dma(n), dma(dp * per), dma(dp * n), dma(dp * n),
            ],
            compiler_params=pltpu.CompilerParams(
                collective_id=0, has_side_effects=True, vmem_limit_bytes=62 * 1024 * 1024),
        )(member[:, 0], tokens.reshape(n, rows, feat), cotangent.reshape(n, rows, cw), w, down[0], up[0])
        return out, gdown[None], gup[None]

    return jax.shard_map(
        shards,
        mesh=mesh,
        in_specs=(P("dp", "tensor"), P("dp", "tensor"), P("tensor", None), P("tensor", None, None),
                  P("tensor", None, None), P("dp", None)),
        out_specs=(P(("dp", "tensor"), None), P("tensor", None, "dp"), P("tensor", "dp", None)),
        check_vma=False,
    )
```

```python
import functools

import jax
import jax.numpy as jnp
from jax import lax
from jax.experimental import pallas as pl
from jax.experimental.pallas import tpu as pltpu
from jax.sharding import PartitionSpec as P

BLK = 128
SCALE = 2.0
TRAIL = (((1,), (1,)), ((), ()))
LEAD = (((0,), (0,)), ((), ()))
F32 = jnp.float32
BF16 = jnp.bfloat16


def kernel(n, dp, member, tok_h, cot_h, w_h, down_h, up_h, out, gdown, gup,
           tok, cot_t, w, down, up, cot, dw, uw, bs, bx, br, ss, sx, sr, hb, gs, gx, gr, us, ur,
           in_s, wd_s, wd_r, wu_s, wu_r, fd_s, fd_r, fu_s, fu_r, bx_s, bx_r, bz_s, bz_r,
           sx_s, sx_r, sz_s, sz_r, h_s, h_r, gx_s, gx_r, g_s, g_r, u_s, u_r):
    d = lax.axis_index("dp")
    j = lax.axis_index("tensor")
    total = dp * n
    lin = d * n + j
    _, rows, feat = tok.shape
    cw = cot.shape[2]
    rank, width = up.shape
    half = rank // 2
    per = n // dp
    nz = n // 2
    core = d % 2
    mate = d + 1 - 2 * core
    px = j % 2
    zme = j // 2
    partner = j + 1 - 2 * px
    blocks = member.shape[0]
    mine = pl.ds(pl.multiple_of(core * half, half), half)
    other = pl.ds(pl.multiple_of((1 - core) * half, half), half)

    def rcopy(src, dst, s, r, dd, tt):
        return pltpu.make_async_remote_copy(
            src_ref=src, dst_ref=dst, send_sem=s, recv_sem=r,
            device_id={"dp": dd, "tensor": tt}, device_id_type=pl.DeviceIdType.MESH)

    def loop(lo, hi, fn):
        def step(k, c):
            fn(k)
            return c
        lax.fori_loop(lo, hi, step, 0)

    barrier = pltpu.get_barrier_semaphore()

    def greet(o):
        t = (lin + o) % total
        pl.semaphore_signal(barrier, inc=1, device_id={"dp": t // n, "tensor": t % n},
                            device_id_type=pl.DeviceIdType.MESH)

    loads = [pltpu.make_async_copy(a, b, in_s.at[k]) for k, (a, b) in enumerate(
        ((down_h, down), (up_h, up), (w_h, w), (tok_h, tok), (cot_h, cot_t)))]
    for one in loads:
        one.start()
    loop(1, total, greet)
    for one in loads:
        one.wait()
    dw[j] = down[:, pl.ds(pl.multiple_of(j * feat, feat), feat)]
    uw[j] = up[...]

    def base(i):
        bs[i] = jnp.dot(tok[i], w[...], preferred_element_type=F32).astype(BF16)

    loop(0, nz, lambda z: base(2 * z + 1 - px))
    pl.semaphore_wait(barrier, total - 1)

    def down_copy(o):
        t = (j + o) % n
        return rcopy(down.at[mine, pl.ds(pl.multiple_of(t * feat, feat), feat)], dw.at[j, mine],
                     wd_s.at[o], wd_r.at[o], d, t)

    def up_copy(o):
        t = (j + o) % n
        return rcopy(up.at[mine], uw.at[j, mine], wu_s.at[o], wu_r.at[o], d, t)

    def bx_copy(z):
        return rcopy(bs.at[2 * z + 1 - px], bx.at[z], bx_s.at[z], bx_r.at[z], d, partner)

    loop(1, n, lambda o: down_copy(o).start())
    loop(1, n, lambda o: up_copy(o).start())
    loop(0, nz, lambda z: bx_copy(z).start())
    loop(0, nz, lambda z: base(2 * z + px))

    if rows % 16 == 0:
        cot[...] = cot_t[...].T.reshape(n, rows, cw)
    else:
        cot[...] = cot_t[...].astype(F32).T.reshape(n, rows, cw).astype(BF16)

    def fdown(o, part):
        s = (j + n - o) % n
        return rcopy(dw.at[s, part], dw.at[s, part], fd_s.at[o], fd_r.at[o], mate, j)

    def fup(o, part):
        s = (j + n - o) % n
        return rcopy(uw.at[s, part], uw.at[s, part], fu_s.at[o], fu_r.at[o], mate, j)

    def got_down(o):
        s = (j + n - o) % n
        rcopy(dw.at[s, mine], dw.at[s, mine], wd_s.at[o], wd_r.at[o], d, s).wait_recv()
        fdown(o, mine).start()

    def got_up(o):
        s = (j + n - o) % n
        rcopy(uw.at[s, mine], uw.at[s, mine], wu_s.at[o], wu_r.at[o], d, s).wait_recv()
        fup(o, mine).start()

    loop(1, n, got_down)
    loop(1, n, got_up)

    def z_copy(ref, dst, s_sem, r_sem, o):
        t = 2 * ((zme + o) % nz) + px
        return rcopy(ref.at[t], dst.at[zme], s_sem.at[o], r_sem.at[o], d, t)

    def z_wait(dst, s_sem, r_sem, o):
        s = (zme + nz - o) % nz
        rcopy(dst.at[s], dst.at[s], s_sem.at[o], r_sem.at[o], d, 2 * s + px).wait_recv()

    def base_join(o):
        z = (zme + o) % nz
        bx_copy(z).wait_recv()
        i = 2 * z + px
        bs[i] = (bs[i].astype(F32) + bx[z].astype(F32)).astype(BF16)

    def base_send(o):
        base_join(o)
        z_copy(bs, br, bz_s, bz_r, o).start()

    loop(1, nz, base_send)
    base_join(0)

    loop(1, n, lambda o: fdown(o, other).wait_recv())
    loop(1, n, lambda o: fup(o, other).wait_recv())

    pick = (lax.broadcasted_iota(jnp.int32, (width, cw), 0)
            == lax.broadcasted_iota(jnp.int32, (width, cw), 1) + j * cw).astype(BF16)

    def owners(i):
        k0 = (i * rows) // BLK
        k1 = (i * rows + rows - 1) // BLK
        return member[k0], member[k1], (k0 + 1) * BLK - i * rows

    def split(x):
        hi = x.astype(BF16)
        return hi, (x - hi.astype(F32)).astype(BF16)

    def partial(i):
        m0, m1, edge = owners(i)
        first = lax.broadcasted_iota(jnp.int32, (rows, rank), 0) < edge
        pair = jnp.concatenate([dw[m0], dw[m1]], axis=0)
        hs = lax.dot_general(tok[i], pair, TRAIL, preferred_element_type=F32)
        upair = jnp.concatenate([uw[m0], uw[m1]], axis=0)
        uj = jnp.dot(upair, pick, preferred_element_type=F32).astype(BF16)
        cs = SCALE * lax.dot_general(cot[i], uj, TRAIL, preferred_element_type=F32)
        h = jnp.where(first, hs[:, :rank], hs[:, rank:])
        b = jnp.where(first, cs[:, :rank], cs[:, rank:])
        ss[i] = jnp.concatenate([*split(h), *split(b)], axis=1)

    def merged(x):
        return (x[:, :rank] + x[:, rank:2 * rank], x[:, 2 * rank:3 * rank] + x[:, 3 * rank:])

    def sx_copy(z):
        return rcopy(ss.at[2 * z + 1 - px], sx.at[z], sx_s.at[z], sx_r.at[z], d, partner)

    def partial_send(o):
        z = (zme + o) % nz
        partial(2 * z + 1 - px)
        sx_copy(z).start()

    loop(1, nz + 1, partial_send)
    loop(0, nz, lambda z: partial(2 * z + px))

    def side_join(o):
        z = (zme + o) % nz
        sx_copy(z).wait_recv()
        i = 2 * z + px
        h, b = merged(ss[i].astype(F32) + sx[z].astype(F32))
        ss[i] = jnp.concatenate([*split(h), *split(b)], axis=1)

    def side_send(o):
        side_join(o)
        z_copy(ss, sr, sz_s, sz_r, o).start()

    loop(1, nz, side_send)
    side_join(0)
    sr[zme] = ss[j]
    loop(1, nz, lambda o: z_wait(sr, sz_s, sz_r, o))
    hidden, back = merged(sum(sr[s].astype(F32) for s in range(nz)))
    hidden, back = hidden.astype(BF16), back.astype(BF16)
    hb[j] = jnp.concatenate([hidden, back], axis=1)

    def hb_copy(o):
        return rcopy(hb.at[j], hb.at[j], h_s.at[o], h_r.at[o], d, (j + o) % n)

    loop(1, n, lambda o: hb_copy(o).start())

    def flat(x):
        if rows % 16 == 0:
            return x.reshape(n * rows, x.shape[2])
        return x.astype(F32).reshape(n * rows, x.shape[2]).astype(BF16)

    span = n * rank
    row_block = lax.broadcasted_iota(jnp.int32, (n * rows, 1), 0) // BLK
    row_member = jnp.zeros((n * rows, 1), jnp.int32)
    for k in range(blocks):
        row_member = jnp.where(row_block == k, member[k], row_member)

    def hb_recv(o):
        s = (j + n - o) % n
        rcopy(hb.at[s], hb.at[s], h_s.at[o], h_r.at[o], d, s).wait_recv()

    loop(1, n, hb_recv)
    both = flat(hb[...])

    def spread(offset, lo, size):
        keep = lax.broadcasted_iota(jnp.int32, (n * rows, size), 1) // rank + lo == row_member
        ra = lax.broadcasted_iota(jnp.int32, (2 * rank, size), 0)
        rb = lax.broadcasted_iota(jnp.int32, (2 * rank, size), 1) % rank
        tiled = jnp.dot(both, (ra == rb + offset).astype(BF16), preferred_element_type=F32)
        return jnp.where(keep, tiled, 0.0).astype(BF16)

    def grads_of(lo):
        g = lax.dot_general(spread(rank, lo, nz * rank), flat(tok[...]), LEAD, preferred_element_type=F32)
        return g.reshape(nz, rank, feat)

    def gx_copy(k):
        return rcopy(gs.at[k], gx.at[k], gx_s.at[k], gx_r.at[k], mate, j)

    gs[0:nz] = grads_of((1 - core) * nz).astype(BF16)
    loop(0, nz, lambda k: gx_copy(k).start())
    gs[nz:n] = grads_of(core * nz).astype(BF16)

    dd, slot = j // per, (d // 2) * per + j % per

    def gd_copy(k):
        return rcopy(gs.at[nz + k], gr.at[slot], g_s.at[k], g_r.at[slot], dd, core * nz + k)

    def not_me(k):
        return jnp.logical_or(dd != d, core * nz + k != j)

    def gd_start(k):
        gx_copy(k).wait_recv()
        gs[nz + k] = (gs[nz + k].astype(F32) + gx[k].astype(F32)).astype(BF16)

        @pl.when(not_me(k))
        def _():
            gd_copy(k).start()

    loop(0, nz, gd_start)

    @pl.when(jnp.logical_and(dd == d, j // nz == core))
    def _():
        gr[slot] = gs[nz + j % nz]

    gu = (SCALE * lax.dot_general(spread(0, 0, span), flat(cot[...]), LEAD, preferred_element_type=F32))
    gu = gu.reshape(n, rank, cw)
    part = rank // dp
    for k in range(dp):
        us[:, k] = gu[:, k * part:(k + 1) * part, :]

    def gu_copy(o):
        t = (lin + o) % total
        return rcopy(us.at[t % n, t // n], ur.at[d, j], u_s.at[o], u_r.at[o], t // n, t % n)

    loop(1, total, lambda o: gu_copy(o).start())
    ur[d, j] = us[j, d]

    m0, m1, edge = owners(j)
    a0 = SCALE * jnp.dot(hidden, uw[m0], preferred_element_type=F32)
    a1 = SCALE * jnp.dot(hidden, uw[m1], preferred_element_type=F32)
    first = lax.broadcasted_iota(jnp.int32, (rows, width), 0) < edge
    adapter = jnp.where(first, a0, a1).astype(BF16).astype(F32)
    br[zme] = bs[j]
    loop(1, nz, lambda o: z_wait(br, bz_s, bz_r, o))
    out[...] = (sum(br[s].astype(F32) for s in range(nz)) + adapter).astype(BF16)

    ny = dp // 2

    def gd_recv(k):
        sd, sj = 2 * (k // per) + j // nz, d * per + k % per

        @pl.when(jnp.logical_or(sd != d, sj != j))
        def _():
            rcopy(gr.at[k], gr.at[k], g_s.at[0], g_r.at[k], sd, sj).wait_recv()

    loop(0, ny * per, gd_recv)
    for q in range(per):
        gdown[:, q * feat:(q + 1) * feat] = sum(gr[k * per + q].astype(F32) for k in range(ny))

    def gu_recv(o):
        s = (lin + total - o) % total
        rcopy(ur.at[s // n, s % n], ur.at[s // n, s % n], u_s.at[o], u_r.at[o], s // n, s % n).wait_recv()

    loop(1, total, gu_recv)
    gup[...] = jnp.concatenate([sum(ur[k, t] for k in range(dp)) for t in range(n)], axis=1)

    def drain(o):
        down_copy(o).wait_send()
        up_copy(o).wait_send()
        fdown(o, mine).wait_send()
        fup(o, mine).wait_send()
        hb_copy(o).wait_send()

    loop(1, n, drain)

    def drain_pair(z):
        bx_copy(z).wait_send()
        sx_copy(z).wait_send()
        gx_copy(z).wait_send()

    loop(0, nz, drain_pair)

    def drain_z(o):
        z_copy(bs, br, bz_s, bz_r, o).wait_send()
        z_copy(ss, sr, sz_s, sz_r, o).wait_send()

    loop(1, nz, drain_z)

    def gd_drain(k):
        @pl.when(not_me(k))
        def _():
            gd_copy(k).wait_send()

    loop(0, nz, gd_drain)
    loop(1, total, lambda o: gu_copy(o).wait_send())


def solution(mesh):
    dp, n = mesh.shape["dp"], mesh.shape["tensor"]

    def shards(tokens, cotangent, w, down, up, member):
        rows, feat = tokens.shape[0] // n, tokens.shape[1]
        cw, width, rank = cotangent.shape[1], w.shape[1], up.shape[1]
        per, nz = n // dp, n // 2
        vmem = pl.BlockSpec(memory_space=pltpu.VMEM)
        dma = lambda k: pltpu.SemaphoreType.DMA((k,))
        out, gdown, gup = pl.pallas_call(
            functools.partial(kernel, n, dp),
            out_shape=(
                jax.ShapeDtypeStruct((rows, width), BF16),
                jax.ShapeDtypeStruct((rank, per * feat), F32),
                jax.ShapeDtypeStruct((rank // dp, width), F32),
            ),
            in_specs=[pl.BlockSpec(memory_space=pltpu.SMEM)] + [pl.BlockSpec(memory_space=pl.ANY)] * 5,
            out_specs=(vmem,) * 3,
            scratch_shapes=[
                pltpu.VMEM((n, rows, feat), BF16),
                pltpu.VMEM((cw, n * rows), BF16),
                pltpu.VMEM((feat, width), BF16),
                pltpu.VMEM((rank, n * feat), BF16),
                pltpu.VMEM((rank, width), BF16),
                pltpu.VMEM((n, rows, cw), BF16),
                pltpu.VMEM((n, rank, feat), BF16),
                pltpu.VMEM((n, rank, width), BF16),
                pltpu.VMEM((n, rows, width), BF16),
                pltpu.VMEM((nz, rows, width), BF16),
                pltpu.VMEM((nz, rows, width), BF16),
                pltpu.VMEM((n, rows, 4 * rank), BF16),
                pltpu.VMEM((nz, rows, 4 * rank), BF16),
                pltpu.VMEM((nz, rows, 4 * rank), BF16),
                pltpu.VMEM((n, rows, 2 * rank), BF16),
                pltpu.VMEM((n, rank, feat), BF16),
                pltpu.VMEM((nz, rank, feat), BF16),
                pltpu.VMEM((dp // 2 * per, rank, feat), BF16),
                pltpu.VMEM((n, dp, rank // dp, cw), F32),
                pltpu.VMEM((dp, n, rank // dp, cw), F32),
                dma(5),
                *[dma(n) for _ in range(8)],
                *[dma(nz) for _ in range(8)],
                dma(n), dma(n), dma(nz), dma(nz), dma(nz), dma(dp // 2 * per),
                dma(dp * n), dma(dp * n),
            ],
            compiler_params=pltpu.CompilerParams(
                collective_id=0, has_side_effects=True, vmem_limit_bytes=62 * 1024 * 1024),
        )(member[:, 0], tokens.reshape(n, rows, feat), cotangent.T, w, down[0], up[0])
        return out, gdown[None], gup[None]

    return jax.shard_map(
        shards,
        mesh=mesh,
        in_specs=(P("dp", "tensor"), P("dp", "tensor"), P("tensor", None), P("tensor", None, None),
                  P("tensor", None, None), P("dp", None)),
        out_specs=(P(("dp", "tensor"), None), P("tensor", None, "dp"), P("tensor", "dp", None)),
        check_vma=False,
    )
```
